256 devices in a mesh: seq: 64 (over y, z, x_hi), mp: 4 (over x_lo, core).
Axes of the slice: x: 4 (x_hi: 2, x_lo: 2; x = x_hi * 2 + x_lo), y: 4, z: 8, core: 2. Of those that a mesh axis runs over, the one named last changes fastest.
Arguments:
- stream: bfloat16 [20480, 1024], P('seq'), as said below
- gain_attn: float32 [1024], replicated, may hold values from 0.1 to 1.9
- gain_mlp: float32 [1024], replicated, may hold values from 0.1 to 1.9
- gain_read: float32 [1024], replicated, may hold values from 0.1 to 1.9
- query_weight: bfloat16 [1024, 1024], P(None, 'mp'), as said below
- key_weight: bfloat16 [1024, 1024], P(None, 'mp'), as said below
- value_weight: bfloat16 [1024, 1024], P(None, 'mp'), may hold values from -0.1875 to 0.1875
- out_weight: bfloat16 [1024, 1024], P('mp'), may hold values from -0.1875 to 0.1875
- up_weight: bfloat16 [1024, 2048], P(None, 'mp'), may hold values from -0.1875 to 0.1875
- down_weight: bfloat16 [2048, 1024], P('mp'), may hold values from -0.125 to 0.125
- read_weight: bfloat16 [1024, 8192], P(None, 'mp'), may hold values from -0.1875 to 0.1875
- read_bias: float32 [8192], P('mp'), may hold values from -3 to 3
- spike_counts: int32 [20480, 8192], P('seq', 'mp'), may hold values from 0 to 7
Outputs:
- log_rate: bfloat16 [20480, 8192], P('seq', 'mp')
- poisson_loss: float32 [20480], P('seq')
The draws below stay inside these ranges and needn't reach their ends.
Inputs may be any that keep to these rules, and one draw needn't show every extreme that they name: Real-valued residual stream. `query_weight`: Real-valued projection. `key_weight`: Real-valued projection.
All inputs are finite; a program needn't handle non-finite values.
Results may differ from the reference program's by a relative error of at most 0.014.
Values may be sent and summed in bfloat16 or wider, within the bound.
A program may use at most 128 MiB of HBM per device.

```python
import jax
import jax.numpy as jnp
from jax import lax

D = 1024
H = 16
DH = 64
FF = 2048
NEU = 8192
TOKENS = 20480


def projection_parts(key):
    base = jnp.clip(jax.random.normal(jax.random.fold_in(key, 11), (D, H * DH), jnp.float32), -6.0, 6.0)
    noise = jnp.clip(jax.random.normal(jax.random.fold_in(key, 12), (D, H * DH), jnp.float32), -6.0, 6.0)
    return (base, noise)


def draw_query_weight(key, part):
    base, noise = projection_parts(key)
    factor = (3.0 / D) ** 0.5
    return (base * factor).astype(jnp.bfloat16)


def draw_key_weight(key, part):
    base, noise = projection_parts(key)
    factor = (3.0 / D) ** 0.5
    return (noise * factor).astype(jnp.bfloat16)


def draw_stream(key, part):
    return jnp.clip(jax.random.normal(jax.random.fold_in(key, 24), (TOKENS, D), jnp.float32), -6.0, 6.0).astype(jnp.bfloat16)


def place_ends(drawn, stream_key, smallest, largest):
    longest = drawn.shape.index(max(drawn.shape))
    spots = []
    for shift in (0, 1):
        where = [jax.random.randint(jax.random.fold_in(stream_key, axis), (), 0, length) for axis, length in enumerate(drawn.shape)]
        where[longest] = (where[longest] + shift) % drawn.shape[longest]
        spots.append(tuple(where))
    return drawn.at[spots[0]].set(smallest).at[spots[1]].set(largest)


def level_of(key, dims, split, low, largest):
    factor_of = 1.0
    for position, shards_of in split:
        steps = jax.random.uniform(jax.random.fold_in(jax.random.fold_in(key, 6), position), (shards_of,), jnp.float32, low / len(split), largest / len(split))
        factor_of = factor_of * jnp.repeat(jnp.exp(steps), dims[position] // shards_of).reshape((-1,) + (1,) * (len(dims) - 1 - position))
    return factor_of


def scatter_about(stream_key, shape, width, most, pieces=(), held_as=jnp.bfloat16):
    entries = jax.random.normal(stream_key, shape, jnp.float32) * width
    if len(pieces) > 0:
        entries = level_of(stream_key, shape, pieces, -0.22, 0.18) * entries
    return jnp.clip(entries, min=-most, max=most).astype(held_as)


def setup_inputs(seed: int = 0) -> dict:
    splits = jax.random.split(jax.random.key(seed), 14)
    return {
        "stream": draw_stream(jax.random.fold_in(splits[13], 71), 0),
        "gain_attn": jnp.clip(1.0 + 0.18 * jax.random.normal(splits[1], (D,), jnp.float32), 0.1, 1.9),
        "gain_mlp": jnp.clip(1.0 + 0.18 * jax.random.normal(splits[2], (D,), jnp.float32), 0.1, 1.9),
        "gain_read": jnp.clip(1.0 + 0.18 * jax.random.normal(splits[3], (D,), jnp.float32), 0.1, 1.9),
        "query_weight": draw_query_weight(jax.random.fold_in(splits[13], 71), 0),
        "key_weight": draw_key_weight(jax.random.fold_in(splits[13], 71), 0),
        "value_weight": scatter_about(splits[6], (D, H * DH), D ** -0.5, 0.1875, ((1, 4),)),
        "out_weight": scatter_about(splits[7], (H * DH, D), (H * DH) ** -0.5, 0.1875, ((0, 4),)),
        "up_weight": scatter_about(splits[8], (D, FF), D ** -0.5, 0.1875, ((1, 4),)),
        "down_weight": scatter_about(splits[9], (FF, D), FF ** -0.5, 0.125, ((0, 4),)),
        "read_weight": scatter_about(splits[10], (D, NEU), D ** -0.5, 0.1875, ((1, 4),)),
        "read_bias": scatter_about(splits[11], (NEU,), 0.5, 3.0, ((0, 4),), jnp.float32),
        "spike_counts": place_ends(jax.random.randint(splits[12], (TOKENS, NEU), 0, 8), jax.random.fold_in(splits[12], 1), 0, 7).astype(jnp.int32),
    }


def rms_norm(field, gain):
    wide = field.astype(jnp.float32)
    scale = lax.rsqrt(lax.optimization_barrier(jnp.mean(wide * wide, axis=-1, keepdims=True)) + 1e-05)
    return wide * scale * gain.astype(jnp.float32)

def causal_attention(queries, keys, values):
    total = queries.shape[0]
    block_rows = 512
    queries_all = queries.astype(jnp.float32).reshape(total, H, DH)
    keys_all = keys.astype(jnp.float32).reshape(total, H, DH)
    values_all = values.astype(jnp.float32).reshape(total, H, DH)
    factor = DH ** (-0.5)

    def query_block(block_index):
        start = (block_index * block_rows).astype(jnp.int32)
        query_rows = lax.dynamic_slice_in_dim(queries_all, start, block_rows, 0)
        query_pos = start + jnp.arange(block_rows, dtype=jnp.int32)

        def key_step(key_index, state):
            best, total_weight, accum = state
            key_start = (key_index * block_rows).astype(jnp.int32)
            key_rows = lax.dynamic_slice_in_dim(keys_all, key_start, block_rows, 0)
            value_rows = lax.dynamic_slice_in_dim(values_all, key_start, block_rows, 0)
            key_pos = key_start + jnp.arange(block_rows, dtype=jnp.int32)
            scores = jnp.einsum('qhd,khd->hqk', query_rows, key_rows) * factor
            allowed = key_pos[None, None, :] <= query_pos[None, :, None]
            scores = jnp.where(allowed, scores, -1e+30)
            fresh = jnp.maximum(best, lax.optimization_barrier(jnp.max(scores, axis=-1)))
            weights = jnp.where(allowed, jnp.exp(scores - fresh[..., None]), 0.0)
            decay = jnp.exp(best - fresh)
            total_weight = total_weight * decay + lax.optimization_barrier(jnp.sum(weights, axis=-1))
            weights_low = lax.optimization_barrier(weights.astype(jnp.bfloat16))
            accum = accum * decay[..., None] + jnp.einsum('hqk,khd->hqd', weights_low.astype(jnp.float32), value_rows)
            return (fresh, total_weight, accum)
        init = (jnp.full((H, block_rows), -1e+30, jnp.float32), jnp.zeros((H, block_rows), jnp.float32), jnp.zeros((H, block_rows, DH), jnp.float32))
        best, total_weight, accum = lax.fori_loop(0, block_index + 1, key_step, init)
        result = accum / total_weight[..., None]
        return jnp.transpose(result, (1, 0, 2)).reshape(block_rows, H * DH)
    blocks = lax.map(query_block, jnp.arange(total // block_rows, dtype=jnp.int32))
    return blocks.reshape(total, H * DH)

def reference(stream, gain_attn, gain_mlp, gain_read, query_weight, key_weight, value_weight, out_weight, up_weight, down_weight, read_weight, read_bias, spike_counts):
    normed = rms_norm(stream, gain_attn).astype(jnp.bfloat16)
    queries = jnp.dot(normed, query_weight, preferred_element_type=jnp.float32).astype(jnp.bfloat16)
    keys = jnp.dot(normed, key_weight, preferred_element_type=jnp.float32).astype(jnp.bfloat16)
    values = jnp.dot(normed, value_weight, preferred_element_type=jnp.float32).astype(jnp.bfloat16)
    attended = causal_attention(queries, keys, values).astype(jnp.bfloat16)
    resid = (stream.astype(jnp.float32) + jnp.dot(attended, out_weight, preferred_element_type=jnp.float32)).astype(jnp.bfloat16)
    mlp_in = rms_norm(resid, gain_mlp).astype(jnp.bfloat16)
    hidden = jax.nn.gelu(jnp.dot(mlp_in, up_weight, preferred_element_type=jnp.float32), approximate=True).astype(jnp.bfloat16)
    outcome = resid.astype(jnp.float32) + jnp.dot(hidden, down_weight, preferred_element_type=jnp.float32)
    read_in = rms_norm(outcome, gain_read).astype(jnp.bfloat16)
    rate_full = jnp.dot(read_in, read_weight, preferred_element_type=jnp.float32) + read_bias.astype(jnp.float32)
    poisson_loss = lax.optimization_barrier(jnp.mean(jnp.exp(rate_full) - spike_counts.astype(jnp.float32) * rate_full, axis=-1))
    return (rate_full.astype(jnp.bfloat16), poisson_loss)
```

```python
import jax
import jax.numpy as jnp
from jax import lax
from jax.experimental import pallas as pl
from jax.experimental.pallas import tpu as pltpu
from jax.sharding import PartitionSpec as P

NEU = 8192
NY = 4
NZ = 8
ROWS = 640
CHUNK = 128
SUB = 80
WIDE = 1024
LOG2E = 1.4426950408889634
QSCALE = LOG2E * 0.125
LOW = -1e30
MESH = pl.DeviceIdType.MESH
F32 = jnp.float32
BF16 = jnp.bfloat16


def rms(wide, gain):
    scale = lax.rsqrt(jnp.mean(wide * wide, axis=-1, keepdims=True) + 1e-05)
    return wide * scale * gain


def nt_dot(a, b):
    return lax.dot_general(a, b, (((1,), (1,)), ((), ())), preferred_element_type=F32)


def layer_kernel(
    stream,
    gain_attn,
    gain_mlp,
    gain_read,
    wq,
    wk,
    wv,
    wo_own,
    wu_own,
    wd_own,
    out,
    xbuf,
    kvbuf,
    mirror,
    vaug,
    qrx,
    qpad,
    acc,
    best,
    otx,
    orx,
    stx,
    srx,
    att,
    slices,
    wo,
    wu,
    wd,
    rbuf,
    x_send,
    x_recv,
    kv_send,
    kv_recv,
    m_send,
    m_recv,
    q_send,
    q_recv,
    o_send,
    o_recv,
    s_send,
    s_recv,
    a_send,
    a_recv,
    w_local,
    w_send,
    w_recv,
    r_send,
    r_recv,
    l_sem,
):
    seq = lax.axis_index("seq")
    mp = lax.axis_index("mp")
    xh = seq % 2
    z = (seq // 2) % NZ
    y = seq // (2 * NZ)
    xl = mp // 2
    core = mp % 2
    x = 2 * xh + xl

    def at(y_, z_, xh_, mp_):
        return ((y_ * NZ + z_) * 2 + xh_, mp_)

    def along_x(step):
        x_ = (x + step) % 4
        return at(y, z, x_ // 2, (x_ % 2) * 2 + core)

    sibling = at(y, z, xh, xl * 2 + 1 - core)
    across = at(y, z, 1 - xh, (1 - xl) * 2 + core)
    beside = at(y, z, xh, (1 - xl) * 2 + core)
    z_up = at(y, (z + 1) % NZ, xh, mp)
    z_down = at(y, (z + NZ - 1) % NZ, xh, mp)
    mirrored = at(NY - 1 - y, z, xh, mp)

    def remote(src, dst, send, recv, device):
        return pltpu.make_async_remote_copy(
            src_ref=src,
            dst_ref=dst,
            send_sem=send,
            recv_sem=recv,
            device_id=device,
            device_id_type=MESH,
        )

    mine = 4 * xh + mp

    def group_member(step):
        e = (mine + step) % 8
        return e, at(y, z, e // 4, e % 4)

    barrier = pltpu.get_barrier_semaphore()
    for device in (
        [z_up, z_down]
        + [at((y + k) % NY, z, xh, mp) for k in range(1, NY)]
        + [group_member(k)[1] for k in range(1, 8)]
    ):
        pl.semaphore_signal(barrier, inc=1, device_id=device, device_id_type=MESH)
    pl.semaphore_wait(barrier, 12)

    half = ROWS // 4
    own_rows = pl.multiple_of(xh * (ROWS // 2), 16)
    other_rows = pl.multiple_of((1 - xh) * (ROWS // 2), 16)
    my_half = pl.multiple_of(core * half, 16)
    x_cross = remote(
        stream.at[pl.ds(my_half, half)],
        xbuf.at[pl.ds(own_rows + my_half, half)],
        x_send.at[0],
        x_recv.at[0],
        across,
    )
    x_cross.start()
    own = pltpu.make_async_copy(stream, xbuf.at[pl.ds(own_rows, ROWS // 2)], l_sem.at[0])
    own.start()

    weights = ((wo_own, wo), (wu_own, wu), (wd_own, wd))
    w_copies = []
    for i, (src, dst) in enumerate(weights):
        rows = src.shape[0]
        local = pltpu.make_async_copy(src, dst.at[mp], w_local.at[i])
        local.start()
        w_copies.append(local)
        for j, step in enumerate((1, 3)):
            part = pl.ds(j * (rows // 2), rows // 2)
            remote(
                src.at[part], dst.at[mp, part], w_send.at[i, j], w_recv.at[i, j], along_x(step)
            ).start()

    acc[...] = jnp.zeros_like(acc)
    best[...] = jnp.full_like(best, LOW)

    other_half = xbuf.at[pl.ds(other_rows + my_half, half)]
    x_forward = remote(other_half, other_half, x_send.at[1], x_recv.at[1], sibling)
    remote(other_half, other_half, x_send.at[0], x_recv.at[0], across).wait_recv()
    x_forward.start()
    own.wait()
    for i, (src, dst) in enumerate(weights):
        remote(src, dst.at[mp], w_send.at[i, 2], w_recv.at[i, 2], sibling).start()
    rest_half = xbuf.at[pl.ds(other_rows + (half - my_half), half)]
    remote(rest_half, rest_half, x_send.at[1], x_recv.at[1], sibling).wait_recv()

    lane = lax.broadcasted_iota(jnp.int32, (CHUNK, 128), 1)
    first = lane < 64
    columns = pl.ds(pl.multiple_of(xh * 128, 128), 128)
    for r in range(ROWS // CHUNK):
        rows = pl.ds(r * CHUNK, CHUNK)
        normed = rms(xbuf[rows].astype(F32), gain_attn[...]).astype(BF16)
        query = jnp.dot(normed, wq[:, columns], preferred_element_type=F32) * QSCALE
        qrx[y, rows] = query.astype(BF16)
        key = jnp.dot(normed, wk[:, columns], preferred_element_type=F32).T.astype(BF16)
        value = jnp.dot(normed, wv[:, columns], preferred_element_type=F32).T.astype(BF16)
        kvbuf[0, z, 0:64, rows] = key[0:64]
        kvbuf[0, z, 64:128, rows] = value[0:64]
        mirror[0:64, rows] = key[64:128]
        mirror[64:128, rows] = value[64:128]

    def kv_copy(h, slot, direction, d):
        block = kvbuf.at[h, slot]
        device = z_up if direction == 0 else z_down
        return remote(block, block, kv_send.at[h, direction, d], kv_recv.at[h, slot], device)

    m_copy = remote(mirror, kvbuf.at[1, z], m_send, m_recv, mirrored)
    m_copy.start()
    kv_copy(0, z, 0, 0).start()
    kv_copy(0, z, 1, 0).start()
    q_copies = []
    for k in range(1, NY):
        q_copy = remote(
            qrx.at[y], qrx.at[y], q_send.at[k - 1], q_recv.at[y], at((y + k) % NY, z, xh, mp)
        )
        q_copy.start()
        q_copies.append(q_copy)

    def unpack(s):
        for r in range(ROWS // CHUNK):
            rows = pl.ds(r * CHUNK, CHUNK)
            packed = qrx[s, rows].astype(F32)
            qpad[0, s, rows] = jnp.where(first, packed, 0.0).astype(BF16)
            qpad[1, s, rows] = jnp.where(first, pltpu.roll(packed, 64, 1), 0.0).astype(BF16)

    key_row = lax.broadcasted_iota(jnp.int32, (128, ROWS), 0)

    def prepare(h, slot):
        block = kvbuf[h, slot].astype(F32)
        vaug[...] = jnp.where(key_row < 64, 1.0, block).astype(BF16)

    def update(h, slot, s, r, keys, masked):
        rows = pl.ds(r * CHUNK, CHUNK)
        scores = jnp.dot(qpad[h, s, rows], kvbuf[h, slot, :, 0:keys], preferred_element_type=F32)
        if masked:
            query_at = lax.broadcasted_iota(jnp.int32, (CHUNK, keys), 0) + r * CHUNK
            key_at = lax.broadcasted_iota(jnp.int32, (CHUNK, keys), 1)
            scores = jnp.where(key_at <= query_at, scores, LOW)
        before = best[h, s, rows]
        fresh = jnp.maximum(before, jnp.max(scores, axis=1, keepdims=True))
        probs = jnp.exp2(scores - jnp.concatenate([fresh] * (keys // 128), axis=1)).astype(BF16)
        decay = jnp.exp2(before - fresh)
        acc[h, s, rows] = acc[h, s, rows] * decay + nt_dot(probs, vaug[:, 0:keys])
        best[h, s, rows] = fresh

    def diagonal(h, s):
        prepare(h, z)
        for r in range(ROWS // CHUNK):
            update(h, z, s, r, (r + 1) * CHUNK, True)

    def visit(h, slot, start):
        prepare(h, slot)

        def one(s, carry):
            for r in range(ROWS // CHUNK):
                update(h, slot, s, r, ROWS, False)
            return carry

        lax.fori_loop(start, NY, one, 0)

    def row_of(h):
        return y + h * (NY - 1 - 2 * y)

    unpack(y)
    diagonal(0, y)
    m_copy.wait_recv()
    kv_copy(1, z, 0, 0).start()
    kv_copy(1, z, 1, 0).start()
    for k in range(1, NY):
        s = (y + k) % NY
        remote(qrx.at[s], qrx.at[s], q_send.at[k - 1], q_recv.at[s], z_up).wait_recv()
        unpack(s)
    diagonal(1, NY - 1 - y)

    def own_visits(h, carry):
        visit(h, z, row_of(h) + 1)
        return carry

    lax.fori_loop(0, 2, own_visits, 0)

    def ring_step(u, carry):
        d = u // 2 + 1
        h = u % 2
        left = (z + NZ - d) % NZ
        right = (z + d) % NZ
        kv_copy(h, left, 0, 0).wait_recv()

        @pl.when((d < 3) | (h == 0))
        def _():
            kv_copy(h, left, 0, d).start()

        kv_copy(h, right, 1, 0).wait_recv()

        @pl.when((d < 3) | (h == 1))
        def _():
            kv_copy(h, right, 1, d).start()

        row = row_of(h)

        def side(k, carry):
            slot = left + k * (right - left)
            visit(h, slot, row + jnp.where(slot > z, 1, 0))
            return carry

        lax.fori_loop(0, 2, side, 0)
        return carry

    lax.fori_loop(0, 6, ring_step, 0)

    far = (z + NZ // 2) % NZ

    def last_step(h, carry):
        kv_copy(h, far, 0, 0).wait_recv()
        visit(h, far, row_of(h) + jnp.where(far > z, 1, 0))
        return carry

    lax.fori_loop(0, 2, last_step, 0)

    theirs = (1 - xl) * 2 + core
    for i, (src, dst) in enumerate(weights):
        rows = src.shape[0]
        for j, step in enumerate((1, 3)):
            part = pl.ds(j * (rows // 2), rows // 2)
            block = dst.at[theirs, part]
            remote(block, block, w_send.at[i, j], w_recv.at[i, j], sibling).wait_recv()
        remote(
            dst.at[theirs], dst.at[theirs], w_send.at[i, 3], w_recv.at[i, 3], sibling
        ).start()

    def partial(s, values, stats):
        for r in range(ROWS // CHUNK):
            rows = pl.ds(r * CHUNK, CHUNK)
            a0 = acc[0, s, rows]
            a1 = acc[1, s, rows]
            total = jnp.where(first, a0, pltpu.roll(a1, 64, 1))
            numer = jnp.where(first, pltpu.roll(a0, 64, 1), a1)
            some = total > 0.0
            safe = jnp.where(some, total, 1.0)
            values[rows] = (numer / safe).astype(BF16)
            high = jnp.where(first, best[0, s, rows], best[1, s, rows])
            lse = jnp.where(some, high + jnp.log(safe) * LOG2E, LOW).T
            stats[0:8, rows] = lse[0:8]
            stats[8:16, rows] = lse[64:72]

    o_copies = []
    for k in range(1, NY):
        s = (y + k) % NY
        partial(s, otx.at[k - 1], stx.at[k - 1])
        device = at(s, z, xh, mp)
        for copy in (
            remote(otx.at[k - 1], orx.at[y], o_send.at[k - 1], o_recv.at[y], device),
            remote(stx.at[k - 1], srx.at[y], s_send.at[k - 1], s_recv.at[y], device),
        ):
            copy.start()
            o_copies.append(copy)
    partial(y, orx.at[y], srx.at[y])
    for k in range(1, NY):
        s = (y + k) % NY
        remote(orx.at[s], orx.at[s], o_send.at[k - 1], o_recv.at[s], z_up).wait_recv()
        remote(srx.at[s], srx.at[s], s_send.at[k - 1], s_recv.at[s], z_up).wait_recv()
    for r in range(ROWS // CHUNK):
        rows = pl.ds(r * CHUNK, CHUNK)
        lses = []
        for s in range(NY):
            pair = [
                jnp.broadcast_to(srx[s, 8 * h : 8 * h + 1, rows], (64, CHUNK)) for h in range(2)
            ]
            lses.append(jnp.concatenate(pair, axis=0).T)
        top = jnp.maximum(jnp.maximum(lses[0], lses[1]), jnp.maximum(lses[2], lses[3]))
        numer = jnp.zeros((CHUNK, 128), F32)
        denom = jnp.zeros((CHUNK, 128), F32)
        for s in range(NY):
            weight = jnp.exp2(lses[s] - top)
            denom = denom + weight
            numer = numer + weight * orx[s, rows].astype(F32)
        att[rows] = (numer / denom).astype(BF16)

    column = 2 * mp + xh
    a_copies = []
    for k in range(1, 8):
        e, device = group_member(k)
        src = att.at[pl.ds(pl.multiple_of(e * SUB, 16), SUB)]
        copy = remote(src, slices.at[column], a_send.at[k - 1], a_recv.at[column], device)
        copy.start()
        a_copies.append(copy)
    slices[column] = att[pl.ds(pl.multiple_of(mine * SUB, 16), SUB)]
    for k in range(1, 8):
        e = (mine + k) % 8
        source = 2 * (e % 4) + e // 4
        remote(
            slices.at[source], slices.at[source], a_send.at[k - 1], a_recv.at[source], sibling
        ).wait_recv()
    for i, (src, dst) in enumerate(weights):
        w_copies[i].wait()
        near = dst.at[xl * 2 + 1 - core]
        remote(src, near, w_send.at[i, 2], w_recv.at[i, 2], sibling).wait_recv()
        away = dst.at[(1 - xl) * 2 + 1 - core]
        remote(away, away, w_send.at[i, 3], w_recv.at[i, 3], sibling).wait_recv()

    total = stream[pl.ds(pl.multiple_of(mp * SUB, 16), SUB)].astype(F32)
    for m in range(4):
        pair = jnp.concatenate([slices[2 * m], slices[2 * m + 1]], axis=1)
        total = total + jnp.dot(pair, wo[m], preferred_element_type=F32)
    resid = total.astype(BF16).astype(F32)
    mlp_in = rms(resid, gain_mlp[...]).astype(BF16)
    outcome = resid
    for m in range(4):
        hidden = jnp.dot(mlp_in, wu[m], preferred_element_type=F32)
        hidden = jax.nn.gelu(hidden, approximate=True).astype(BF16)
        outcome = outcome + jnp.dot(hidden, wd[m], preferred_element_type=F32)
    rbuf[mp] = rms(outcome, gain_read[...]).astype(BF16)

    def r_copy(slot, i, device):
        return remote(rbuf.at[slot], rbuf.at[slot], r_send.at[i], r_recv.at[i], device)

    r_copy(mp, 0, beside).start()
    r_copy(mp, 1, sibling).start()
    r_copy(theirs, 0, beside).wait_recv()
    r_copy(theirs, 2, sibling).start()
    r_copy(xl * 2 + 1 - core, 1, sibling).wait_recv()
    r_copy((1 - xl) * 2 + 1 - core, 2, sibling).wait_recv()
    for m in range(4):
        out[m * SUB : (m + 1) * SUB] = rbuf[m]

    x_cross.wait_send()
    x_forward.wait_send()
    m_copy.wait_send()
    for copy in q_copies + o_copies + a_copies:
        copy.wait_send()
    for d in range(4):
        for h in range(2):
            for direction in range(2):
                if d < 3 or h == direction:
                    kv_copy(h, z, direction, d).wait_send()
    for i, (src, dst) in enumerate(weights):
        rows = src.shape[0]
        for j in range(2):
            part = pl.ds(j * (rows // 2), rows // 2)
            remote(
                src.at[part], dst.at[mp, part], w_send.at[i, j], w_recv.at[i, j], sibling
            ).wait_send()
        remote(src, dst.at[mp], w_send.at[i, 2], w_recv.at[i, 2], sibling).wait_send()
        remote(
            dst.at[theirs], dst.at[theirs], w_send.at[i, 3], w_recv.at[i, 3], sibling
        ).wait_send()
    r_copy(mp, 0, beside).wait_send()
    r_copy(mp, 1, sibling).wait_send()
    r_copy(theirs, 2, sibling).wait_send()


def read_inputs(stream, gains, wq, wk, wv, wo, wu, wd):
    vmem = pl.BlockSpec(memory_space=pltpu.VMEM)
    hbm = pl.BlockSpec(memory_space=pl.ANY)
    dma = pltpu.SemaphoreType.DMA
    return pl.pallas_call(
        layer_kernel,
        out_shape=jax.ShapeDtypeStruct(stream.shape, BF16),
        in_specs=[vmem] * 7 + [hbm] * 3,
        out_specs=vmem,
        scratch_shapes=[
            pltpu.VMEM((ROWS, WIDE), BF16),
            pltpu.VMEM((2, NZ, 128, ROWS), BF16),
            pltpu.VMEM((128, ROWS), BF16),
            pltpu.VMEM((128, ROWS), BF16),
            pltpu.VMEM((NY, ROWS, 128), BF16),
            pltpu.VMEM((2, NY, ROWS, 128), BF16),
            pltpu.VMEM((2, NY, ROWS, 128), F32),
            pltpu.VMEM((2, NY, ROWS, 128), F32),
            pltpu.VMEM((NY - 1, ROWS, 128), BF16),
            pltpu.VMEM((NY, ROWS, 128), BF16),
            pltpu.VMEM((NY - 1, 16, ROWS), F32),
            pltpu.VMEM((NY, 16, ROWS), F32),
            pltpu.VMEM((ROWS, 128), BF16),
            pltpu.VMEM((8, SUB, 128), BF16),
            pltpu.VMEM((4,) + wo.shape, BF16),
            pltpu.VMEM((4,) + wu.shape, BF16),
            pltpu.VMEM((4,) + wd.shape, BF16),
            pltpu.VMEM((4, SUB, WIDE), BF16),
            dma((2,)),
            dma((2,)),
            dma((2, 2, 4)),
            dma((2, NZ)),
            dma,
            dma,
            dma((NY - 1,)),
            dma((NY,)),
            dma((NY - 1,)),
            dma((NY,)),
            dma((NY - 1,)),
            dma((NY,)),
            dma((7,)),
            dma((8,)),
            dma((3,)),
            dma((3, 4)),
            dma((3, 4)),
            dma((3,)),
            dma((3,)),
            dma((1,)),
        ],
        compiler_params=pltpu.CompilerParams(
            collective_id=0, has_side_effects=True, vmem_limit_bytes=60 * 1024 * 1024
        ),
    )(stream, *gains, wq, wk, wv, wo, wu, wd)


def per_device(
    stream,
    gain_attn,
    gain_mlp,
    gain_read,
    query_weight,
    key_weight,
    value_weight,
    out_weight,
    up_weight,
    down_weight,
    read_weight,
    read_bias,
    spike_counts,
):
    gains = [gain.reshape(1, WIDE) for gain in (gain_attn, gain_mlp, gain_read)]
    read_in = read_inputs(
        stream, gains, query_weight, key_weight, value_weight, out_weight, up_weight, down_weight
    )
    rate_full = jnp.dot(read_in, read_weight, preferred_element_type=F32) + read_bias
    loss_part = jnp.sum(jnp.exp(rate_full) - spike_counts.astype(F32) * rate_full, axis=-1)
    poisson_loss = lax.psum(loss_part, "mp") / NEU
    return (rate_full.astype(BF16), poisson_loss)


def solution(mesh):
    in_specs = (
        P("seq", None),
        P(),
        P(),
        P(),
        P(None, "mp"),
        P(None, "mp"),
        P(None, "mp"),
        P("mp", None),
        P(None, "mp"),
        P("mp", None),
        P(None, "mp"),
        P("mp"),
        P("seq", "mp"),
    )
    out_specs = (P("seq", "mp"), P("seq"))
    return jax.shard_map(
        per_device, mesh=mesh, in_specs=in_specs, out_specs=out_specs, check_vma=False
    )
```

```python
import jax
import jax.numpy as jnp
from jax import lax
from jax.experimental import pallas as pl
from jax.experimental.pallas import tpu as pltpu
from jax.sharding import PartitionSpec as P

NEU = 8192
NY = 4
NZ = 8
ROWS = 640
CHUNK = 128
SUB = 80
WIDE = 1024
TILE = 512
LOG2E = 1.4426950408889634
QSCALE = LOG2E * 0.125
LOW = -1e30
MESH = pl.DeviceIdType.MESH
F32 = jnp.float32
BF16 = jnp.bfloat16


def rms(wide, gain):
    scale = lax.rsqrt(jnp.mean(wide * wide, axis=-1, keepdims=True) + 1e-05)
    return wide * scale * gain


def nt_dot(a, b):
    return lax.dot_general(a, b, (((1,), (1,)), ((), ())), preferred_element_type=F32)


def layer_kernel(
    gain_attn,
    gain_mlp,
    gain_read,
    bias,
    stream,
    wq_own,
    wk_own,
    wv_own,
    wo_own,
    wu_own,
    wd_own,
    read_own,
    spikes_own,
    out,
    loss,
    wq,
    wk,
    wv,
    wread,
    spikes,
    read_in,
    terms,
    lossbuf,
    xbuf,
    kvbuf,
    mirror,
    vaug,
    qrx,
    qpad,
    acc,
    best,
    otx,
    orx,
    stx,
    srx,
    att,
    slices,
    wo,
    wu,
    wd,
    rbuf,
    x_send,
    x_recv,
    kv_send,
    kv_recv,
    m_send,
    m_recv,
    q_send,
    q_recv,
    o_send,
    o_recv,
    s_send,
    s_recv,
    a_send,
    a_recv,
    w_local,
    w_send,
    w_recv,
    r_send,
    r_recv,
    t_send,
    t_recv,
    l_sem,
):
    seq = lax.axis_index("seq")
    mp = lax.axis_index("mp")
    xh = seq % 2
    z = (seq // 2) % NZ
    y = seq // (2 * NZ)
    xl = mp // 2
    core = mp % 2
    x = 2 * xh + xl

    def at(y_, z_, xh_, mp_):
        return ((y_ * NZ + z_) * 2 + xh_, mp_)

    def along_x(step):
        x_ = (x + step) % 4
        return at(y, z, x_ // 2, (x_ % 2) * 2 + core)

    sibling = at(y, z, xh, xl * 2 + 1 - core)
    across = at(y, z, 1 - xh, (1 - xl) * 2 + core)
    beside = at(y, z, xh, (1 - xl) * 2 + core)
    z_up = at(y, (z + 1) % NZ, xh, mp)
    z_down = at(y, (z + NZ - 1) % NZ, xh, mp)
    mirrored = at(NY - 1 - y, z, xh, mp)

    def remote(src, dst, send, recv, device):
        return pltpu.make_async_remote_copy(
            src_ref=src,
            dst_ref=dst,
            send_sem=send,
            recv_sem=recv,
            device_id=device,
            device_id_type=MESH,
        )

    mine = 4 * xh + mp

    def group_member(step):
        e = (mine + step) % 8
        return e, at(y, z, e // 4, e % 4)

    columns = pl.ds(pl.multiple_of(xh * 128, 128), 128)
    early = []
    for i, (src, dst) in enumerate(((wq_own, wq), (wk_own, wk), (wv_own, wv))):
        copy = pltpu.make_async_copy(src.at[:, columns], dst, l_sem.at[1 + i])
        copy.start()
        early.append(copy)
    own_rows = pl.multiple_of(xh * (ROWS // 2), 16)
    own = pltpu.make_async_copy(stream, xbuf.at[pl.ds(own_rows, ROWS // 2)], l_sem.at[0])
    own.start()

    barrier = pltpu.get_barrier_semaphore()
    for device in (
        [z_up, z_down]
        + [at((y + k) % NY, z, xh, mp) for k in range(1, NY)]
        + [group_member(k)[1] for k in range(1, 8)]
    ):
        pl.semaphore_signal(barrier, inc=1, device_id=device, device_id_type=MESH)
    pl.semaphore_wait(barrier, 12)

    half = ROWS // 4
    other_rows = pl.multiple_of((1 - xh) * (ROWS // 2), 16)
    my_half = pl.multiple_of(core * half, 16)
    x_cross = remote(
        stream.at[pl.ds(my_half, half)],
        xbuf.at[pl.ds(own_rows + my_half, half)],
        x_send.at[0],
        x_recv.at[0],
        across,
    )
    x_cross.start()

    weights = ((wo_own, wo), (wu_own, wu), (wd_own, wd))
    w_copies = []
    for i, (src, dst) in enumerate(weights):
        rows = src.shape[0]
        local = pltpu.make_async_copy(src, dst.at[mp], w_local.at[i])
        local.start()
        w_copies.append(local)
        for j, step in enumerate((1, 3)):
            part = pl.ds(j * (rows // 2), rows // 2)
            remote(
                src.at[part], dst.at[mp, part], w_send.at[i, j], w_recv.at[i, j], along_x(step)
            ).start()

    acc[...] = jnp.zeros_like(acc)
    best[...] = jnp.full_like(best, LOW)

    other_half = xbuf.at[pl.ds(other_rows + my_half, half)]
    x_forward = remote(other_half, other_half, x_send.at[1], x_recv.at[1], sibling)
    remote(other_half, other_half, x_send.at[0], x_recv.at[0], across).wait_recv()
    x_forward.start()
    own.wait()
    for i, (src, dst) in enumerate(weights):
        remote(src, dst.at[mp], w_send.at[i, 2], w_recv.at[i, 2], sibling).start()
    rest_half = xbuf.at[pl.ds(other_rows + (half - my_half), half)]
    remote(rest_half, rest_half, x_send.at[1], x_recv.at[1], sibling).wait_recv()

    lane = lax.broadcasted_iota(jnp.int32, (CHUNK, 128), 1)
    first = lane < 64
    for copy in early:
        copy.wait()
    for r in range(ROWS // CHUNK):
        rows = pl.ds(r * CHUNK, CHUNK)
        normed = rms(xbuf[rows].astype(F32), gain_attn[...]).astype(BF16)
        query = jnp.dot(normed, wq[...], preferred_element_type=F32) * QSCALE
        qrx[y, rows] = query.astype(BF16)
        key = jnp.dot(normed, wk[...], preferred_element_type=F32).T.astype(BF16)
        value = jnp.dot(normed, wv[...], preferred_element_type=F32).T.astype(BF16)
        kvbuf[0, z, 0:64, rows] = key[0:64]
        kvbuf[0, z, 64:128, rows] = value[0:64]
        mirror[0:64, rows] = key[64:128]
        mirror[64:128, rows] = value[64:128]

    def kv_copy(h, slot, direction, d):
        block = kvbuf.at[h, slot]
        device = z_up if direction == 0 else z_down
        return remote(block, block, kv_send.at[h, direction, d], kv_recv.at[h, slot], device)

    m_copy = remote(mirror, kvbuf.at[1, z], m_send, m_recv, mirrored)
    m_copy.start()
    kv_copy(0, z, 0, 0).start()
    kv_copy(0, z, 1, 0).start()
    q_copies = []
    for k in range(1, NY):
        q_copy = remote(
            qrx.at[y], qrx.at[y], q_send.at[k - 1], q_recv.at[y], at((y + k) % NY, z, xh, mp)
        )
        q_copy.start()
        q_copies.append(q_copy)

    late = [
        pltpu.make_async_copy(read_own, wread, l_sem.at[4]),
        pltpu.make_async_copy(spikes_own, spikes, l_sem.at[5]),
    ]
    for copy in late:
        copy.start()

    def unpack(s):
        for r in range(ROWS // CHUNK):
            rows = pl.ds(r * CHUNK, CHUNK)
            packed = qrx[s, rows].astype(F32)
            qpad[0, s, rows] = jnp.where(first, packed, 0.0).astype(BF16)
            qpad[1, s, rows] = jnp.where(first, pltpu.roll(packed, 64, 1), 0.0).astype(BF16)

    key_row = lax.broadcasted_iota(jnp.int32, (128, ROWS), 0)

    def prepare(h, slot):
        block = kvbuf[h, slot].astype(F32)
        vaug[...] = jnp.where(key_row < 64, 1.0, block).astype(BF16)

    def update(h, slot, s, r, keys, masked):
        rows = pl.ds(r * CHUNK, CHUNK)
        scores = jnp.dot(qpad[h, s, rows], kvbuf[h, slot, :, 0:keys], preferred_element_type=F32)
        if masked:
            query_at = lax.broadcasted_iota(jnp.int32, (CHUNK, keys), 0) + r * CHUNK
            key_at = lax.broadcasted_iota(jnp.int32, (CHUNK, keys), 1)
            scores = jnp.where(key_at <= query_at, scores, LOW)
        before = best[h, s, rows]
        fresh = jnp.maximum(before, jnp.max(scores, axis=1, keepdims=True))
        probs = jnp.exp2(scores - jnp.concatenate([fresh] * (keys // 128), axis=1)).astype(BF16)
        decay = jnp.exp2(before - fresh)
        acc[h, s, rows] = acc[h, s, rows] * decay + nt_dot(probs, vaug[:, 0:keys])
        best[h, s, rows] = fresh

    def diagonal(h, s):
        prepare(h, z)
        for r in range(ROWS // CHUNK):
            update(h, z, s, r, (r + 1) * CHUNK, True)

    def visit(h, slot, start):
        prepare(h, slot)

        def one(s, carry):
            for r in range(ROWS // CHUNK):
                update(h, slot, s, r, ROWS, False)
            return carry

        lax.fori_loop(start, NY, one, 0)

    def row_of(h):
        return y + h * (NY - 1 - 2 * y)

    unpack(y)
    diagonal(0, y)
    m_copy.wait_recv()
    kv_copy(1, z, 0, 0).start()
    kv_copy(1, z, 1, 0).start()
    for k in range(1, NY):
        s = (y + k) % NY
        remote(qrx.at[s], qrx.at[s], q_send.at[k - 1], q_recv.at[s], z_up).wait_recv()
        unpack(s)
    diagonal(1, NY - 1 - y)

    def own_visits(h, carry):
        visit(h, z, row_of(h) + 1)
        return carry

    lax.fori_loop(0, 2, own_visits, 0)

    def ring_step(u, carry):
        d = u // 2 + 1
        h = u % 2
        left = (z + NZ - d) % NZ
        right = (z + d) % NZ
        kv_copy(h, left, 0, 0).wait_recv()

        @pl.when((d < 3) | (h == 0))
        def _():
            kv_copy(h, left, 0, d).start()

        kv_copy(h, right, 1, 0).wait_recv()

        @pl.when((d < 3) | (h == 1))
        def _():
            kv_copy(h, right, 1, d).start()

        row = row_of(h)

        def side(k, carry):
            slot = left + k * (right - left)
            visit(h, slot, row + jnp.where(slot > z, 1, 0))
            return carry

        lax.fori_loop(0, 2, side, 0)
        return carry

    lax.fori_loop(0, 6, ring_step, 0)

    far = (z + NZ // 2) % NZ

    def last_step(h, carry):
        kv_copy(h, far, 0, 0).wait_recv()
        visit(h, far, row_of(h) + jnp.where(far > z, 1, 0))
        return carry

    lax.fori_loop(0, 2, last_step, 0)

    theirs = (1 - xl) * 2 + core
    for i, (src, dst) in enumerate(weights):
        rows = src.shape[0]
        for j, step in enumerate((1, 3)):
            part = pl.ds(j * (rows // 2), rows // 2)
            block = dst.at[theirs, part]
            remote(block, block, w_send.at[i, j], w_recv.at[i, j], sibling).wait_recv()
        remote(
            dst.at[theirs], dst.at[theirs], w_send.at[i, 3], w_recv.at[i, 3], sibling
        ).start()

    def partial(s, values, stats):
        for r in range(ROWS // CHUNK):
            rows = pl.ds(r * CHUNK, CHUNK)
            a0 = acc[0, s, rows]
            a1 = acc[1, s, rows]
            total = jnp.where(first, a0, pltpu.roll(a1, 64, 1))
            numer = jnp.where(first, pltpu.roll(a0, 64, 1), a1)
            some = total > 0.0
            safe = jnp.where(some, total, 1.0)
            values[rows] = (numer / safe).astype(BF16)
            high = jnp.where(first, best[0, s, rows], best[1, s, rows])
            lse = jnp.where(some, high + jnp.log(safe) * LOG2E, LOW).T
            stats[0:8, rows] = lse[0:8]
            stats[8:16, rows] = lse[64:72]

    o_copies = []
    for k in range(1, NY):
        s = (y + k) % NY
        partial(s, otx.at[k - 1], stx.at[k - 1])
        device = at(s, z, xh, mp)
        for copy in (
            remote(otx.at[k - 1], orx.at[y], o_send.at[k - 1], o_recv.at[y], device),
            remote(stx.at[k - 1], srx.at[y], s_send.at[k - 1], s_recv.at[y], device),
        ):
            copy.start()
            o_copies.append(copy)
    partial(y, orx.at[y], srx.at[y])
    for k in range(1, NY):
        s = (y + k) % NY
        remote(orx.at[s], orx.at[s], o_send.at[k - 1], o_recv.at[s], z_up).wait_recv()
        remote(srx.at[s], srx.at[s], s_send.at[k - 1], s_recv.at[s], z_up).wait_recv()
    for r in range(ROWS // CHUNK):
        rows = pl.ds(r * CHUNK, CHUNK)
        lses = []
        for s in range(NY):
            pair = [
                jnp.broadcast_to(srx[s, 8 * h : 8 * h + 1, rows], (64, CHUNK)) for h in range(2)
            ]
            lses.append(jnp.concatenate(pair, axis=0).T)
        top = jnp.maximum(jnp.maximum(lses[0], lses[1]), jnp.maximum(lses[2], lses[3]))
        numer = jnp.zeros((CHUNK, 128), F32)
        denom = jnp.zeros((CHUNK, 128), F32)
        for s in range(NY):
            weight = jnp.exp2(lses[s] - top)
            denom = denom + weight
            numer = numer + weight * orx[s, rows].astype(F32)
        att[rows] = (numer / denom).astype(BF16)

    column = 2 * mp + xh
    a_copies = []
    for k in range(1, 8):
        e, device = group_member(k)
        src = att.at[pl.ds(pl.multiple_of(e * SUB, 16), SUB)]
        copy = remote(src, slices.at[column], a_send.at[k - 1], a_recv.at[column], device)
        copy.start()
        a_copies.append(copy)
    slices[column] = att[pl.ds(pl.multiple_of(mine * SUB, 16), SUB)]
    for k in range(1, 8):
        e = (mine + k) % 8
        source = 2 * (e % 4) + e // 4
        remote(
            slices.at[source], slices.at[source], a_send.at[k - 1], a_recv.at[source], sibling
        ).wait_recv()
    for i, (src, dst) in enumerate(weights):
        w_copies[i].wait()
        near = dst.at[xl * 2 + 1 - core]
        remote(src, near, w_send.at[i, 2], w_recv.at[i, 2], sibling).wait_recv()
        away = dst.at[(1 - xl) * 2 + 1 - core]
        remote(away, away, w_send.at[i, 3], w_recv.at[i, 3], sibling).wait_recv()

    total = xbuf[pl.ds(pl.multiple_of(own_rows + mp * SUB, 16), SUB)].astype(F32)
    for m in range(4):
        pair = jnp.concatenate([slices[2 * m], slices[2 * m + 1]], axis=1)
        total = total + jnp.dot(pair, wo[m], preferred_element_type=F32)
    resid = total.astype(BF16).astype(F32)
    mlp_in = rms(resid, gain_mlp[...]).astype(BF16)
    outcome = resid
    for m in range(4):
        hidden = jnp.dot(mlp_in, wu[m], preferred_element_type=F32)
        hidden = jax.nn.gelu(hidden, approximate=True).astype(BF16)
        outcome = outcome + jnp.dot(hidden, wd[m], preferred_element_type=F32)
    rbuf[mp] = rms(outcome, gain_read[...]).astype(BF16)

    def r_copy(slot, i, device):
        return remote(rbuf.at[slot], rbuf.at[slot], r_send.at[i], r_recv.at[i], device)

    r_copy(mp, 0, beside).start()
    r_copy(mp, 1, sibling).start()
    r_copy(theirs, 0, beside).wait_recv()
    r_copy(theirs, 2, sibling).start()
    r_copy(xl * 2 + 1 - core, 1, sibling).wait_recv()
    r_copy((1 - xl) * 2 + 1 - core, 2, sibling).wait_recv()
    for m in range(4):
        read_in[m * SUB : (m + 1) * SUB] = rbuf[m]
    for copy in late:
        copy.wait()

    terms[...] = jnp.zeros_like(terms)

    def readout(t, carry):
        tile = pl.ds(pl.multiple_of(t * TILE, TILE), TILE)
        rate = jnp.dot(read_in[...], wread[:, tile], preferred_element_type=F32) + bias[:, tile]
        out[:, tile] = rate.astype(BF16)
        term = jnp.exp(rate) - spikes[:, tile].astype(F32) * rate
        folded = term[:, 0:128]
        for i in range(1, TILE // 128):
            folded = folded + term[:, i * 128 : (i + 1) * 128]
        terms[0 : 4 * SUB] = terms[0 : 4 * SUB] + folded
        return carry

    lax.fori_loop(0, wread.shape[1] // TILE, readout, 0)
    for r in range(3):
        rows = pl.ds(r * 128, 128)
        part = jnp.sum(terms[rows].T, axis=0, keepdims=True)
        lossbuf[mp, :, rows] = jnp.broadcast_to(part, (8, 128))
    t_copies = []
    for k in range(1, 4):
        copy = remote(
            lossbuf.at[mp], lossbuf.at[mp], t_send.at[k - 1], t_recv.at[mp], at(y, z, xh, (mp + k) % 4)
        )
        copy.start()
        t_copies.append(copy)
    for k in range(1, 4):
        m = (mp + k) % 4
        remote(lossbuf.at[m], lossbuf.at[m], t_send.at[k - 1], t_recv.at[m], sibling).wait_recv()
    summed = (lossbuf[0] + lossbuf[1]) + (lossbuf[2] + lossbuf[3])
    loss[...] = summed[0:1, 0 : 4 * SUB] / NEU

    x_cross.wait_send()
    x_forward.wait_send()
    m_copy.wait_send()
    for copy in q_copies + o_copies + a_copies + t_copies:
        copy.wait_send()
    for d in range(4):
        for h in range(2):
            for direction in range(2):
                if d < 3 or h == direction:
                    kv_copy(h, z, direction, d).wait_send()
    for i, (src, dst) in enumerate(weights):
        rows = src.shape[0]
        for j in range(2):
            part = pl.ds(j * (rows // 2), rows // 2)
            remote(
                src.at[part], dst.at[mp, part], w_send.at[i, j], w_recv.at[i, j], sibling
            ).wait_send()
        remote(src, dst.at[mp], w_send.at[i, 2], w_recv.at[i, 2], sibling).wait_send()
        remote(
            dst.at[theirs], dst.at[theirs], w_send.at[i, 3], w_recv.at[i, 3], sibling
        ).wait_send()
    r_copy(mp, 0, beside).wait_send()
    r_copy(mp, 1, sibling).wait_send()
    r_copy(theirs, 2, sibling).wait_send()


def layer(gains, bias, stream, wq, wk, wv, wo, wu, wd, read_weight, spikes):
    vmem = pl.BlockSpec(memory_space=pltpu.VMEM)
    hbm = pl.BlockSpec(memory_space=pl.ANY)
    dma = pltpu.SemaphoreType.DMA
    return pl.pallas_call(
        layer_kernel,
        out_shape=(
            jax.ShapeDtypeStruct(spikes.shape, BF16),
            jax.ShapeDtypeStruct((1, spikes.shape[0]), F32),
        ),
        in_specs=[vmem] * 4 + [hbm] * 9,
        out_specs=(vmem, vmem),
        scratch_shapes=[
            pltpu.VMEM((WIDE, 128), BF16),
            pltpu.VMEM((WIDE, 128), BF16),
            pltpu.VMEM((WIDE, 128), BF16),
            pltpu.VMEM(read_weight.shape, BF16),
            pltpu.VMEM(spikes.shape, jnp.int32),
            pltpu.VMEM(stream.shape, BF16),
            pltpu.VMEM((384, 128), F32),
            pltpu.VMEM((4, 8, 384), F32),
            pltpu.VMEM((ROWS, WIDE), BF16),
            pltpu.VMEM((2, NZ, 128, ROWS), BF16),
            pltpu.VMEM((128, ROWS), BF16),
            pltpu.VMEM((128, ROWS), BF16),
            pltpu.VMEM((NY, ROWS, 128), BF16),
            pltpu.VMEM((2, NY, ROWS, 128), BF16),
            pltpu.VMEM((2, NY, ROWS, 128), F32),
            pltpu.VMEM((2, NY, ROWS, 128), F32),
            pltpu.VMEM((NY - 1, ROWS, 128), BF16),
            pltpu.VMEM((NY, ROWS, 128), BF16),
            pltpu.VMEM((NY - 1, 16, ROWS), F32),
            pltpu.VMEM((NY, 16, ROWS), F32),
            pltpu.VMEM((ROWS, 128), BF16),
            pltpu.VMEM((8, SUB, 128), BF16),
            pltpu.VMEM((4,) + wo.shape, BF16),
            pltpu.VMEM((4,) + wu.shape, BF16),
            pltpu.VMEM((4,) + wd.shape, BF16),
            pltpu.VMEM((4, SUB, WIDE), BF16),
            dma((2,)),
            dma((2,)),
            dma((2, 2, 4)),
            dma((2, NZ)),
            dma,
            dma,
            dma((NY - 1,)),
            dma((NY,)),
            dma((NY - 1,)),
            dma((NY,)),
            dma((NY - 1,)),
            dma((NY,)),
            dma((7,)),
            dma((8,)),
            dma((3,)),
            dma((3, 4)),
            dma((3, 4)),
            dma((3,)),
            dma((3,)),
            dma((3,)),
            dma((4,)),
            dma((6,)),
        ],
        compiler_params=pltpu.CompilerParams(
            collective_id=0, has_side_effects=True, vmem_limit_bytes=60 * 1024 * 1024
        ),
    )(*gains, bias, stream, wq, wk, wv, wo, wu, wd, read_weight, spikes)


def per_device(
    stream,
    gain_attn,
    gain_mlp,
    gain_read,
    query_weight,
    key_weight,
    value_weight,
    out_weight,
    up_weight,
    down_weight,
    read_weight,
    read_bias,
    spike_counts,
):
    gains = [gain.reshape(1, WIDE) for gain in (gain_attn, gain_mlp, gain_read)]
    log_rate, poisson_loss = layer(
        gains,
        read_bias.reshape(1, -1),
        stream,
        query_weight,
        key_weight,
        value_weight,
        out_weight,
        up_weight,
        down_weight,
        read_weight,
        spike_counts,
    )
    return (log_rate, poisson_loss.reshape(-1))


def solution(mesh):
    in_specs = (
        P("seq", None),
        P(),
        P(),
        P(),
        P(None, "mp"),
        P(None, "mp"),
        P(None, "mp"),
        P("mp", None),
        P(None, "mp"),
        P("mp", None),
        P(None, "mp"),
        P("mp"),
        P("seq", "mp"),
    )
    out_specs = (P("seq", "mp"), P("seq"))
    return jax.shard_map(
        per_device, mesh=mesh, in_specs=in_specs, out_specs=out_specs, check_vma=False
    )
```

```python
import jax
import jax.numpy as jnp
from jax import lax
from jax.experimental import pallas as pl
from jax.experimental.pallas import tpu as pltpu
from jax.sharding import PartitionSpec as P

NEU = 8192
NY = 4
NZ = 8
ROWS = 640
CHUNK = 128
BAND = 320
SUB = 80
WIDE = 1024
TILE = 512
LOG2E = 1.4426950408889634
QSCALE = LOG2E * 0.125
LOW = -1e30
MESH = pl.DeviceIdType.MESH
F32 = jnp.float32
BF16 = jnp.bfloat16


def rms(wide, gain):
    scale = lax.rsqrt(jnp.mean(wide * wide, axis=-1, keepdims=True) + 1e-05)
    return wide * scale * gain


def nt_dot(a, b):
    return lax.dot_general(a, b, (((1,), (1,)), ((), ())), preferred_element_type=F32)


def layer_kernel(
    gain_attn,
    gain_mlp,
    gain_read,
    bias,
    stream,
    wq_own,
    wk_own,
    wv_own,
    wo_own,
    wu_own,
    wd_own,
    read_own,
    spikes_own,
    out,
    loss,
    wq,
    wk,
    wv,
    wread,
    spikes,
    read_in,
    terms,
    lossbuf,
    xbuf,
    kvbuf,
    mirror,
    vaug,
    qrx,
    qpad,
    acc,
    best,
    otx,
    orx,
    stx,
    srx,
    att,
    slices,
    wo,
    wu,
    wd,
    rbuf,
    x_send,
    x_recv,
    kv_send,
    kv_recv,
    m_send,
    m_recv,
    q_send,
    q_recv,
    o_send,
    o_recv,
    s_send,
    s_recv,
    a_send,
    a_recv,
    w_local,
    w_send,
    w_recv,
    r_send,
    r_recv,
    t_send,
    t_recv,
    l_sem,
):
    seq = lax.axis_index("seq")
    mp = lax.axis_index("mp")
    xh = seq % 2
    z = (seq // 2) % NZ
    y = seq // (2 * NZ)
    xl = mp // 2
    core = mp % 2
    x = 2 * xh + xl

    def at(y_, z_, xh_, mp_):
        return ((y_ * NZ + z_) * 2 + xh_, mp_)

    def along_x(step):
        x_ = (x + step) % 4
        return at(y, z, x_ // 2, (x_ % 2) * 2 + core)

    sibling = at(y, z, xh, xl * 2 + 1 - core)
    across = at(y, z, 1 - xh, (1 - xl) * 2 + core)
    beside = at(y, z, xh, (1 - xl) * 2 + core)
    z_up = at(y, (z + 1) % NZ, xh, mp)
    z_down = at(y, (z + NZ - 1) % NZ, xh, mp)
    mirrored = at(NY - 1 - y, z, xh, mp)

    def remote(src, dst, send, recv, device):
        return pltpu.make_async_remote_copy(
            src_ref=src,
            dst_ref=dst,
            send_sem=send,
            recv_sem=recv,
            device_id=device,
            device_id_type=MESH,
        )

    mine = 4 * xh + mp

    def group_member(step):
        e = (mine + step) % 8
        return e, at(y, z, e // 4, e % 4)

    columns = pl.ds(pl.multiple_of(xh * 128, 128), 128)
    early = []
    for i, (src, dst) in enumerate(((wq_own, wq), (wk_own, wk), (wv_own, wv))):
        copy = pltpu.make_async_copy(src.at[:, columns], dst, l_sem.at[1 + i])
        copy.start()
        early.append(copy)
    own_rows = pl.multiple_of(xh * (ROWS // 2), 16)
    own = pltpu.make_async_copy(stream, xbuf.at[pl.ds(own_rows, ROWS // 2)], l_sem.at[0])
    own.start()

    barrier = pltpu.get_barrier_semaphore()
    for device in (
        [z_up, z_down]
        + [at((y + k) % NY, z, xh, mp) for k in range(1, NY)]
        + [group_member(k)[1] for k in range(1, 8)]
    ):
        pl.semaphore_signal(barrier, inc=1, device_id=device, device_id_type=MESH)
    pl.semaphore_wait(barrier, 12)

    half = ROWS // 4
    other_rows = pl.multiple_of((1 - xh) * (ROWS // 2), 16)
    my_half = pl.multiple_of(core * half, 16)
    x_cross = remote(
        stream.at[pl.ds(my_half, half)],
        xbuf.at[pl.ds(own_rows + my_half, half)],
        x_send.at[0],
        x_recv.at[0],
        across,
    )
    x_cross.start()

    weights = ((wo_own, wo), (wu_own, wu), (wd_own, wd))
    w_copies = []
    for i, (src, dst) in enumerate(weights):
        rows = src.shape[0]
        local = pltpu.make_async_copy(src, dst.at[mp], w_local.at[i])
        local.start()
        w_copies.append(local)
        for j, step in enumerate((1, 3)):
            part = pl.ds(j * (rows // 2), rows // 2)
            remote(
                src.at[part], dst.at[mp, part], w_send.at[i, j], w_recv.at[i, j], along_x(step)
            ).start()

    acc[...] = jnp.zeros_like(acc)
    best[...] = jnp.full_like(best, LOW)

    other_half = xbuf.at[pl.ds(other_rows + my_half, half)]
    x_forward = remote(other_half, other_half, x_send.at[1], x_recv.at[1], sibling)
    remote(other_half, other_half, x_send.at[0], x_recv.at[0], across).wait_recv()
    x_forward.start()
    own.wait()
    for i, (src, dst) in enumerate(weights):
        remote(src, dst.at[mp], w_send.at[i, 2], w_recv.at[i, 2], sibling).start()
    rest_half = xbuf.at[pl.ds(other_rows + (half - my_half), half)]
    remote(rest_half, rest_half, x_send.at[1], x_recv.at[1], sibling).wait_recv()

    lane = lax.broadcasted_iota(jnp.int32, (CHUNK, 128), 1)
    first = lane < 64
    for copy in early:
        copy.wait()
    for r in range(ROWS // CHUNK):
        rows = pl.ds(r * CHUNK, CHUNK)
        normed = rms(xbuf[rows].astype(F32), gain_attn[...]).astype(BF16)
        query = jnp.dot(normed, wq[...], preferred_element_type=F32) * QSCALE
        qrx[y, rows] = query.astype(BF16)
        key = jnp.dot(normed, wk[...], preferred_element_type=F32).T.astype(BF16)
        value = jnp.dot(normed, wv[...], preferred_element_type=F32).T.astype(BF16)
        kvbuf[0, z, 0:64, rows] = key[0:64]
        kvbuf[0, z, 64:128, rows] = value[0:64]
        mirror[0:64, rows] = key[64:128]
        mirror[64:128, rows] = value[64:128]

    def kv_copy(h, slot, direction, d):
        block = kvbuf.at[h, slot]
        device = z_up if direction == 0 else z_down
        return remote(block, block, kv_send.at[h, direction, d], kv_recv.at[h, slot], device)

    m_copy = remote(mirror, kvbuf.at[1, z], m_send, m_recv, mirrored)
    m_copy.start()
    kv_copy(0, z, 0, 0).start()
    kv_copy(0, z, 1, 0).start()
    q_copies = []
    for k in range(1, NY):
        q_copy = remote(
            qrx.at[y], qrx.at[y], q_send.at[k - 1], q_recv.at[y], at((y + k) % NY, z, xh, mp)
        )
        q_copy.start()
        q_copies.append(q_copy)

    late = [
        pltpu.make_async_copy(read_own, wread, l_sem.at[4]),
        pltpu.make_async_copy(spikes_own, spikes, l_sem.at[5]),
    ]
    for copy in late:
        copy.start()

    def unpack(s):
        for r in range(ROWS // CHUNK):
            rows = pl.ds(r * CHUNK, CHUNK)
            packed = qrx[s, rows].astype(F32)
            qpad[0, s, rows] = jnp.where(first, packed, 0.0).astype(BF16)
            qpad[1, s, rows] = jnp.where(first, pltpu.roll(packed, 64, 1), 0.0).astype(BF16)

    key_row = lax.broadcasted_iota(jnp.int32, (128, ROWS), 0)

    def prepare(h, slot):
        block = kvbuf[h, slot].astype(F32)
        vaug[...] = jnp.where(key_row < 64, 1.0, block).astype(BF16)

    def update(h, slot, s, r, size, keys, masked):
        rows = pl.ds(r * size, size)
        scores = jnp.dot(qpad[h, s, rows], kvbuf[h, slot, :, 0:keys], preferred_element_type=F32)
        if masked:
            query_at = lax.broadcasted_iota(jnp.int32, (size, keys), 0) + r * size
            key_at = lax.broadcasted_iota(jnp.int32, (size, keys), 1)
            scores = jnp.where(key_at <= query_at, scores, LOW)
        before = best[h, s, rows]
        fresh = jnp.maximum(before, jnp.max(scores, axis=1, keepdims=True))
        probs = jnp.exp2(scores - jnp.concatenate([fresh] * (keys // 128), axis=1)).astype(BF16)
        decay = jnp.exp2(before - fresh)
        acc[h, s, rows] = acc[h, s, rows] * decay + nt_dot(probs, vaug[:, 0:keys])
        best[h, s, rows] = fresh

    def diagonal(h, s):
        prepare(h, z)
        for r in range(ROWS // CHUNK):
            update(h, z, s, r, CHUNK, (r + 1) * CHUNK, True)

    def visit(h, slot, start):
        prepare(h, slot)

        def one(s, carry):
            for r in range(ROWS // BAND):
                update(h, slot, s, r, BAND, ROWS, False)
            return carry

        lax.fori_loop(start, NY, one, 0)

    def row_of(h):
        return y + h * (NY - 1 - 2 * y)

    unpack(y)
    diagonal(0, y)
    m_copy.wait_recv()
    kv_copy(1, z, 0, 0).start()
    kv_copy(1, z, 1, 0).start()
    for k in range(1, NY):
        s = (y + k) % NY
        remote(qrx.at[s], qrx.at[s], q_send.at[k - 1], q_recv.at[s], z_up).wait_recv()
        unpack(s)
    diagonal(1, NY - 1 - y)

    def own_visits(h, carry):
        visit(h, z, row_of(h) + 1)
        return carry

    lax.fori_loop(0, 2, own_visits, 0)

    def ring_step(u, carry):
        d = u // 2 + 1
        h = u % 2
        left = (z + NZ - d) % NZ
        right = (z + d) % NZ
        kv_copy(h, left, 0, 0).wait_recv()

        @pl.when((d < 3) | (h == 0))
        def _():
            kv_copy(h, left, 0, d).start()

        kv_copy(h, right, 1, 0).wait_recv()

        @pl.when((d < 3) | (h == 1))
        def _():
            kv_copy(h, right, 1, d).start()

        row = row_of(h)

        def side(k, carry):
            slot = left + k * (right - left)
            visit(h, slot, row + jnp.where(slot > z, 1, 0))
            return carry

        lax.fori_loop(0, 2, side, 0)
        return carry

    lax.fori_loop(0, 6, ring_step, 0)

    far = (z + NZ // 2) % NZ

    def last_step(h, carry):
        kv_copy(h, far, 0, 0).wait_recv()
        visit(h, far, row_of(h) + jnp.where(far > z, 1, 0))
        return carry

    lax.fori_loop(0, 2, last_step, 0)

    theirs = (1 - xl) * 2 + core
    for i, (src, dst) in enumerate(weights):
        rows = src.shape[0]
        for j, step in enumerate((1, 3)):
            part = pl.ds(j * (rows // 2), rows // 2)
            block = dst.at[theirs, part]
            remote(block, block, w_send.at[i, j], w_recv.at[i, j], sibling).wait_recv()
        remote(
            dst.at[theirs], dst.at[theirs], w_send.at[i, 3], w_recv.at[i, 3], sibling
        ).start()

    def partial(s, values, stats):
        for r in range(ROWS // CHUNK):
            rows = pl.ds(r * CHUNK, CHUNK)
            a0 = acc[0, s, rows]
            a1 = acc[1, s, rows]
            total = jnp.where(first, a0, pltpu.roll(a1, 64, 1))
            numer = jnp.where(first, pltpu.roll(a0, 64, 1), a1)
            some = total > 0.0
            safe = jnp.where(some, total, 1.0)
            values[rows] = (numer / safe).astype(BF16)
            high = jnp.where(first, best[0, s, rows], best[1, s, rows])
            lse = jnp.where(some, high + jnp.log(safe) * LOG2E, LOW).T
            stats[0:8, rows] = lse[0:8]
            stats[8:16, rows] = lse[64:72]

    o_copies = []
    for k in range(1, NY):
        s = (y + k) % NY
        partial(s, otx.at[k - 1], stx.at[k - 1])
        device = at(s, z, xh, mp)
        for copy in (
            remote(otx.at[k - 1], orx.at[y], o_send.at[k - 1], o_recv.at[y], device),
            remote(stx.at[k - 1], srx.at[y], s_send.at[k - 1], s_recv.at[y], device),
        ):
            copy.start()
            o_copies.append(copy)
    partial(y, orx.at[y], srx.at[y])
    for k in range(1, NY):
        s = (y + k) % NY
        remote(orx.at[s], orx.at[s], o_send.at[k - 1], o_recv.at[s], z_up).wait_recv()
        remote(srx.at[s], srx.at[s], s_send.at[k - 1], s_recv.at[s], z_up).wait_recv()
    for r in range(ROWS // CHUNK):
        rows = pl.ds(r * CHUNK, CHUNK)
        lses = []
        for s in range(NY):
            pair = [
                jnp.broadcast_to(srx[s, 8 * h : 8 * h + 1, rows], (64, CHUNK)) for h in range(2)
            ]
            lses.append(jnp.concatenate(pair, axis=0).T)
        top = jnp.maximum(jnp.maximum(lses[0], lses[1]), jnp.maximum(lses[2], lses[3]))
        numer = jnp.zeros((CHUNK, 128), F32)
        denom = jnp.zeros((CHUNK, 128), F32)
        for s in range(NY):
            weight = jnp.exp2(lses[s] - top)
            denom = denom + weight
            numer = numer + weight * orx[s, rows].astype(F32)
        att[rows] = (numer / denom).astype(BF16)

    column = 2 * mp + xh
    a_copies = []
    for k in range(1, 8):
        e, device = group_member(k)
        src = att.at[pl.ds(pl.multiple_of(e * SUB, 16), SUB)]
        copy = remote(src, slices.at[column], a_send.at[k - 1], a_recv.at[column], device)
        copy.start()
        a_copies.append(copy)
    slices[column] = att[pl.ds(pl.multiple_of(mine * SUB, 16), SUB)]
    for k in range(1, 8):
        e = (mine + k) % 8
        source = 2 * (e % 4) + e // 4
        remote(
            slices.at[source], slices.at[source], a_send.at[k - 1], a_recv.at[source], sibling
        ).wait_recv()
    for i, (src, dst) in enumerate(weights):
        w_copies[i].wait()
        near = dst.at[xl * 2 + 1 - core]
        remote(src, near, w_send.at[i, 2], w_recv.at[i, 2], sibling).wait_recv()
        away = dst.at[(1 - xl) * 2 + 1 - core]
        remote(away, away, w_send.at[i, 3], w_recv.at[i, 3], sibling).wait_recv()

    total = xbuf[pl.ds(pl.multiple_of(own_rows + mp * SUB, 16), SUB)].astype(F32)
    for m in range(4):
        pair = jnp.concatenate([slices[2 * m], slices[2 * m + 1]], axis=1)
        total = total + jnp.dot(pair, wo[m], preferred_element_type=F32)
    resid = total.astype(BF16).astype(F32)
    mlp_in = rms(resid, gain_mlp[...]).astype(BF16)
    outcome = resid
    for m in range(4):
        hidden = jnp.dot(mlp_in, wu[m], preferred_element_type=F32)
        hidden = jax.nn.gelu(hidden, approximate=True).astype(BF16)
        outcome = outcome + jnp.dot(hidden, wd[m], preferred_element_type=F32)
    rbuf[mp] = rms(outcome, gain_read[...]).astype(BF16)

    def r_copy(slot, i, device):
        return remote(rbuf.at[slot], rbuf.at[slot], r_send.at[i], r_recv.at[i], device)

    r_copy(mp, 0, beside).start()
    r_copy(mp, 1, sibling).start()
    r_copy(xl * 2 + 1 - core, 1, sibling).wait_recv()
    for copy in late:
        copy.wait()
    terms[...] = jnp.zeros_like(terms)

    def readout(chip):
        rows = pl.ds(pl.multiple_of(chip * (2 * SUB), 32), 2 * SUB)
        read_in[...] = jnp.concatenate([rbuf[2 * chip], rbuf[2 * chip + 1]], axis=0)

        def columns_of(t, carry):
            tile = pl.ds(pl.multiple_of(t * TILE, TILE), TILE)
            rate = jnp.dot(read_in[...], wread[:, tile], preferred_element_type=F32)
            rate = rate + bias[:, tile]
            out[rows, tile] = rate.astype(BF16)
            term = jnp.exp(rate) - spikes[rows, tile].astype(F32) * rate
            folded = term[:, 0:128]
            for i in range(1, TILE // 128):
                folded = folded + term[:, i * 128 : (i + 1) * 128]
            terms[rows] = terms[rows] + folded
            return carry

        lax.fori_loop(0, wread.shape[1] // TILE, columns_of, 0)

    readout(xl)
    r_copy(theirs, 0, beside).wait_recv()
    r_copy(theirs, 2, sibling).start()
    r_copy((1 - xl) * 2 + 1 - core, 2, sibling).wait_recv()
    readout(1 - xl)
    for r in range(3):
        rows = pl.ds(r * 128, 128)
        part = jnp.sum(terms[rows].T, axis=0, keepdims=True)
        lossbuf[mp, :, rows] = jnp.broadcast_to(part, (8, 128))
    t_copies = []
    for k in range(1, 4):
        copy = remote(
            lossbuf.at[mp], lossbuf.at[mp], t_send.at[k - 1], t_recv.at[mp], at(y, z, xh, (mp + k) % 4)
        )
        copy.start()
        t_copies.append(copy)
    for k in range(1, 4):
        m = (mp + k) % 4
        remote(lossbuf.at[m], lossbuf.at[m], t_send.at[k - 1], t_recv.at[m], sibling).wait_recv()
    summed = (lossbuf[0] + lossbuf[1]) + (lossbuf[2] + lossbuf[3])
    loss[...] = summed[0:1, 0 : 4 * SUB] / NEU

    x_cross.wait_send()
    x_forward.wait_send()
    m_copy.wait_send()
    for copy in q_copies + o_copies + a_copies + t_copies:
        copy.wait_send()
    for d in range(4):
        for h in range(2):
            for direction in range(2):
                if d < 3 or h == direction:
                    kv_copy(h, z, direction, d).wait_send()
    for i, (src, dst) in enumerate(weights):
        rows = src.shape[0]
        for j in range(2):
            part = pl.ds(j * (rows // 2), rows // 2)
            remote(
                src.at[part], dst.at[mp, part], w_send.at[i, j], w_recv.at[i, j], sibling
            ).wait_send()
        remote(src, dst.at[mp], w_send.at[i, 2], w_recv.at[i, 2], sibling).wait_send()
        remote(
            dst.at[theirs], dst.at[theirs], w_send.at[i, 3], w_recv.at[i, 3], sibling
        ).wait_send()
    r_copy(mp, 0, beside).wait_send()
    r_copy(mp, 1, sibling).wait_send()
    r_copy(theirs, 2, sibling).wait_send()


def layer(gains, bias, stream, wq, wk, wv, wo, wu, wd, read_weight, spikes):
    vmem = pl.BlockSpec(memory_space=pltpu.VMEM)
    hbm = pl.BlockSpec(memory_space=pl.ANY)
    dma = pltpu.SemaphoreType.DMA
    return pl.pallas_call(
        layer_kernel,
        out_shape=(
            jax.ShapeDtypeStruct(spikes.shape, BF16),
            jax.ShapeDtypeStruct((1, spikes.shape[0]), F32),
        ),
        in_specs=[vmem] * 4 + [hbm] * 9,
        out_specs=(vmem, vmem),
        scratch_shapes=[
            pltpu.VMEM((WIDE, 128), BF16),
            pltpu.VMEM((WIDE, 128), BF16),
            pltpu.VMEM((WIDE, 128), BF16),
            pltpu.VMEM(read_weight.shape, BF16),
            pltpu.VMEM(spikes.shape, jnp.int32),
            pltpu.VMEM((2 * SUB, WIDE), BF16),
            pltpu.VMEM((384, 128), F32),
            pltpu.VMEM((4, 8, 384), F32),
            pltpu.VMEM((ROWS, WIDE), BF16),
            pltpu.VMEM((2, NZ, 128, ROWS), BF16),
            pltpu.VMEM((128, ROWS), BF16),
            pltpu.VMEM((128, ROWS), BF16),
            pltpu.VMEM((NY, ROWS, 128), BF16),
            pltpu.VMEM((2, NY, ROWS, 128), BF16),
            pltpu.VMEM((2, NY, ROWS, 128), F32),
            pltpu.VMEM((2, NY, ROWS, 128), F32),
            pltpu.VMEM((NY - 1, ROWS, 128), BF16),
            pltpu.VMEM((NY, ROWS, 128), BF16),
            pltpu.VMEM((NY - 1, 16, ROWS), F32),
            pltpu.VMEM((NY, 16, ROWS), F32),
            pltpu.VMEM((ROWS, 128), BF16),
            pltpu.VMEM((8, SUB, 128), BF16),
            pltpu.VMEM((4,) + wo.shape, BF16),
            pltpu.VMEM((4,) + wu.shape, BF16),
            pltpu.VMEM((4,) + wd.shape, BF16),
            pltpu.VMEM((4, SUB, WIDE), BF16),
            dma((2,)),
            dma((2,)),
            dma((2, 2, 4)),
            dma((2, NZ)),
            dma,
            dma,
            dma((NY - 1,)),
            dma((NY,)),
            dma((NY - 1,)),
            dma((NY,)),
            dma((NY - 1,)),
            dma((NY,)),
            dma((7,)),
            dma((8,)),
            dma((3,)),
            dma((3, 4)),
            dma((3, 4)),
            dma((3,)),
            dma((3,)),
            dma((3,)),
            dma((4,)),
            dma((6,)),
        ],
        compiler_params=pltpu.CompilerParams(
            collective_id=0, has_side_effects=True, vmem_limit_bytes=60 * 1024 * 1024
        ),
    )(*gains, bias, stream, wq, wk, wv, wo, wu, wd, read_weight, spikes)


def per_device(
    stream,
    gain_attn,
    gain_mlp,
    gain_read,
    query_weight,
    key_weight,
    value_weight,
    out_weight,
    up_weight,
    down_weight,
    read_weight,
    read_bias,
    spike_counts,
):
    gains = [gain.reshape(1, WIDE) for gain in (gain_attn, gain_mlp, gain_read)]
    log_rate, poisson_loss = layer(
        gains,
        read_bias.reshape(1, -1),
        stream,
        query_weight,
        key_weight,
        value_weight,
        out_weight,
        up_weight,
        down_weight,
        read_weight,
        spike_counts,
    )
    return (log_rate, poisson_loss.reshape(-1))


def solution(mesh):
    in_specs = (
        P("seq", None),
        P(),
        P(),
        P(),
        P(None, "mp"),
        P(None, "mp"),
        P(None, "mp"),
        P("mp", None),
        P(None, "mp"),
        P("mp", None),
        P(None, "mp"),
        P("mp"),
        P("seq", "mp"),
    )
    out_specs = (P("seq", "mp"), P("seq"))
    return jax.shard_map(
        per_device, mesh=mesh, in_specs=in_specs, out_specs=out_specs, check_vma=False
    )
```

```python
import jax
import jax.numpy as jnp
from jax import lax
from jax.experimental import pallas as pl
from jax.experimental.pallas import tpu as pltpu
from jax.sharding import PartitionSpec as P

NEU = 8192
NY = 4
NZ = 8
ROWS = 640
CHUNK = 128
BAND = 640
SUB = 80
WIDE = 1024
TILE = 512
LOG2E = 1.4426950408889634
QSCALE = LOG2E * 0.125
LOW = -1e30
MESH = pl.DeviceIdType.MESH
F32 = jnp.float32
BF16 = jnp.bfloat16


def rms(wide, gain):
    scale = lax.rsqrt(jnp.mean(wide * wide, axis=-1, keepdims=True) + 1e-05)
    return wide * scale * gain


def nt_dot(a, b):
    return lax.dot_general(a, b, (((1,), (1,)), ((), ())), preferred_element_type=F32)


def layer_kernel(
    gain_attn,
    gain_mlp,
    gain_read,
    bias,
    stream,
    wq_own,
    wk_own,
    wv_own,
    wo_own,
    wu_own,
    wd_own,
    read_own,
    spikes_own,
    out,
    loss,
    wq,
    wk,
    wv,
    wread,
    spikes,
    read_in,
    terms,
    lossbuf,
    xbuf,
    kvbuf,
    mirror,
    vaug,
    qrx,
    qpad,
    acc,
    best,
    otx,
    orx,
    stx,
    srx,
    att,
    slices,
    wo,
    wu,
    wd,
    rbuf,
    x_send,
    x_recv,
    kv_send,
    kv_recv,
    m_send,
    m_recv,
    q_send,
    q_recv,
    o_send,
    o_recv,
    s_send,
    s_recv,
    a_send,
    a_recv,
    w_local,
    w_send,
    w_recv,
    r_send,
    r_recv,
    t_send,
    t_recv,
    l_sem,
):
    seq = lax.axis_index("seq")
    mp = lax.axis_index("mp")
    xh = seq % 2
    z = (seq // 2) % NZ
    y = seq // (2 * NZ)
    xl = mp // 2
    core = mp % 2
    x = 2 * xh + xl

    def at(y_, z_, xh_, mp_):
        return ((y_ * NZ + z_) * 2 + xh_, mp_)

    def along_x(step):
        x_ = (x + step) % 4
        return at(y, z, x_ // 2, (x_ % 2) * 2 + core)

    sibling = at(y, z, xh, xl * 2 + 1 - core)
    across = at(y, z, 1 - xh, (1 - xl) * 2 + core)
    beside = at(y, z, xh, (1 - xl) * 2 + core)
    z_up = at(y, (z + 1) % NZ, xh, mp)
    z_down = at(y, (z + NZ - 1) % NZ, xh, mp)
    mirrored = at(NY - 1 - y, z, xh, mp)

    def remote(src, dst, send, recv, device):
        return pltpu.make_async_remote_copy(
            src_ref=src,
            dst_ref=dst,
            send_sem=send,
            recv_sem=recv,
            device_id=device,
            device_id_type=MESH,
        )

    mine = 4 * xh + mp

    def group_member(step):
        e = (mine + step) % 8
        return e, at(y, z, e // 4, e % 4)

    columns = pl.ds(pl.multiple_of(xh * 128, 128), 128)
    early = []
    for i, (src, dst) in enumerate(((wq_own, wq), (wk_own, wk), (wv_own, wv))):
        copy = pltpu.make_async_copy(src.at[:, columns], dst, l_sem.at[1 + i])
        copy.start()
        early.append(copy)
    own_rows = pl.multiple_of(xh * (ROWS // 2), 16)
    own = pltpu.make_async_copy(stream, xbuf.at[pl.ds(own_rows, ROWS // 2)], l_sem.at[0])
    own.start()

    barrier = pltpu.get_barrier_semaphore()
    for device in (
        [z_up, z_down]
        + [at((y + k) % NY, z, xh, mp) for k in range(1, NY)]
        + [group_member(k)[1] for k in range(1, 8)]
    ):
        pl.semaphore_signal(barrier, inc=1, device_id=device, device_id_type=MESH)
    pl.semaphore_wait(barrier, 12)

    half = ROWS // 4
    other_rows = pl.multiple_of((1 - xh) * (ROWS // 2), 16)
    my_half = pl.multiple_of(core * half, 16)
    x_cross = remote(
        stream.at[pl.ds(my_half, half)],
        xbuf.at[pl.ds(own_rows + my_half, half)],
        x_send.at[0],
        x_recv.at[0],
        across,
    )
    x_cross.start()

    weights = ((wo_own, wo), (wu_own, wu), (wd_own, wd))
    w_copies = []
    for i, (src, dst) in enumerate(weights):
        rows = src.shape[0]
        local = pltpu.make_async_copy(src, dst.at[mp], w_local.at[i])
        local.start()
        w_copies.append(local)
        for j, step in enumerate((1, 3)):
            part = pl.ds(j * (rows // 2), rows // 2)
            remote(
                src.at[part], dst.at[mp, part], w_send.at[i, j], w_recv.at[i, j], along_x(step)
            ).start()

    acc[...] = jnp.zeros_like(acc)
    best[...] = jnp.full_like(best, LOW)

    other_half = xbuf.at[pl.ds(other_rows + my_half, half)]
    x_forward = remote(other_half, other_half, x_send.at[1], x_recv.at[1], sibling)
    remote(other_half, other_half, x_send.at[0], x_recv.at[0], across).wait_recv()
    x_forward.start()
    own.wait()
    for i, (src, dst) in enumerate(weights):
        remote(src, dst.at[mp], w_send.at[i, 2], w_recv.at[i, 2], sibling).start()
    rest_half = xbuf.at[pl.ds(other_rows + (half - my_half), half)]
    remote(rest_half, rest_half, x_send.at[1], x_recv.at[1], sibling).wait_recv()

    lane = lax.broadcasted_iota(jnp.int32, (CHUNK, 128), 1)
    first = lane < 64
    for copy in early:
        copy.wait()
    for r in range(ROWS // CHUNK):
        rows = pl.ds(r * CHUNK, CHUNK)
        normed = rms(xbuf[rows].astype(F32), gain_attn[...]).astype(BF16)
        query = jnp.dot(normed, wq[...], preferred_element_type=F32) * QSCALE
        qrx[y, rows] = query.astype(BF16)
        key = jnp.dot(normed, wk[...], preferred_element_type=F32).T.astype(BF16)
        value = jnp.dot(normed, wv[...], preferred_element_type=F32).T.astype(BF16)
        kvbuf[0, z, 0:64, rows] = key[0:64]
        kvbuf[0, z, 64:128, rows] = value[0:64]
        mirror[0:64, rows] = key[64:128]
        mirror[64:128, rows] = value[64:128]

    def kv_copy(h, slot, direction, d):
        block = kvbuf.at[h, slot]
        device = z_up if direction == 0 else z_down
        return remote(block, block, kv_send.at[h, direction, d], kv_recv.at[h, slot], device)

    m_copy = remote(mirror, kvbuf.at[1, z], m_send, m_recv, mirrored)
    m_copy.start()
    kv_copy(0, z, 0, 0).start()
    kv_copy(0, z, 1, 0).start()
    q_copies = []
    for k in range(1, NY):
        q_copy = remote(
            qrx.at[y], qrx.at[y], q_send.at[k - 1], q_recv.at[y], at((y + k) % NY, z, xh, mp)
        )
        q_copy.start()
        q_copies.append(q_copy)

    late = [
        pltpu.make_async_copy(read_own, wread, l_sem.at[4]),
        pltpu.make_async_copy(spikes_own, spikes, l_sem.at[5]),
    ]
    for copy in late:
        copy.start()

    def unpack(s):
        for r in range(ROWS // CHUNK):
            rows = pl.ds(r * CHUNK, CHUNK)
            packed = qrx[s, rows].astype(F32)
            qpad[0, s, rows] = jnp.where(first, packed, 0.0).astype(BF16)
            qpad[1, s, rows] = jnp.where(first, pltpu.roll(packed, 64, 1), 0.0).astype(BF16)

    key_row = lax.broadcasted_iota(jnp.int32, (128, ROWS), 0)

    def prepare(h, slot):
        block = kvbuf[h, slot].astype(F32)
        vaug[...] = jnp.where(key_row < 64, 1.0, block).astype(BF16)

    def update(h, slot, s, r, size, keys, masked):
        rows = pl.ds(r * size, size)
        scores = jnp.dot(qpad[h, s, rows], kvbuf[h, slot, :, 0:keys], preferred_element_type=F32)
        if masked:
            query_at = lax.broadcasted_iota(jnp.int32, (size, keys), 0) + r * size
            key_at = lax.broadcasted_iota(jnp.int32, (size, keys), 1)
            scores = jnp.where(key_at <= query_at, scores, LOW)
        before = best[h, s, rows]
        fresh = jnp.maximum(before, jnp.max(scores, axis=1, keepdims=True))
        probs = jnp.exp2(scores - jnp.concatenate([fresh] * (keys // 128), axis=1)).astype(BF16)
        decay = jnp.exp2(before - fresh)
        acc[h, s, rows] = acc[h, s, rows] * decay + nt_dot(probs, vaug[:, 0:keys])
        best[h, s, rows] = fresh

    def diagonal(h, s):
        prepare(h, z)
        update(h, z, s, 0, ROWS // 2, 3 * CHUNK, True)
        update(h, z, s, 1, ROWS // 2, ROWS, True)

    def visit(h, slot, start):
        prepare(h, slot)

        def one(s, carry):
            for r in range(ROWS // BAND):
                update(h, slot, s, r, BAND, ROWS, False)
            return carry

        lax.fori_loop(start, NY, one, 0)

    def row_of(h):
        return y + h * (NY - 1 - 2 * y)

    unpack(y)
    diagonal(0, y)
    m_copy.wait_recv()
    kv_copy(1, z, 0, 0).start()
    kv_copy(1, z, 1, 0).start()
    for k in range(1, NY):
        s = (y + k) % NY
        remote(qrx.at[s], qrx.at[s], q_send.at[k - 1], q_recv.at[s], z_up).wait_recv()
        unpack(s)
    diagonal(1, NY - 1 - y)

    def own_visits(h, carry):
        visit(h, z, row_of(h) + 1)
        return carry

    lax.fori_loop(0, 2, own_visits, 0)

    def ring_step(u, carry):
        d = u // 2 + 1
        h = u % 2
        left = (z + NZ - d) % NZ
        right = (z + d) % NZ
        kv_copy(h, left, 0, 0).wait_recv()

        @pl.when((d < 3) | (h == 0))
        def _():
            kv_copy(h, left, 0, d).start()

        kv_copy(h, right, 1, 0).wait_recv()

        @pl.when((d < 3) | (h == 1))
        def _():
            kv_copy(h, right, 1, d).start()

        row = row_of(h)

        def side(k, carry):
            slot = left + k * (right - left)
            visit(h, slot, row + jnp.where(slot > z, 1, 0))
            return carry

        lax.fori_loop(0, 2, side, 0)
        return carry

    lax.fori_loop(0, 6, ring_step, 0)

    far = (z + NZ // 2) % NZ

    def last_step(h, carry):
        kv_copy(h, far, 0, 0).wait_recv()
        visit(h, far, row_of(h) + jnp.where(far > z, 1, 0))
        return carry

    lax.fori_loop(0, 2, last_step, 0)

    theirs = (1 - xl) * 2 + core
    for i, (src, dst) in enumerate(weights):
        rows = src.shape[0]
        for j, step in enumerate((1, 3)):
            part = pl.ds(j * (rows // 2), rows // 2)
            block = dst.at[theirs, part]
            remote(block, block, w_send.at[i, j], w_recv.at[i, j], sibling).wait_recv()
        remote(
            dst.at[theirs], dst.at[theirs], w_send.at[i, 3], w_recv.at[i, 3], sibling
        ).start()

    def partial(s, values, stats):
        for r in range(ROWS // CHUNK):
            rows = pl.ds(r * CHUNK, CHUNK)
            a0 = acc[0, s, rows]
            a1 = acc[1, s, rows]
            total = jnp.where(first, a0, pltpu.roll(a1, 64, 1))
            numer = jnp.where(first, pltpu.roll(a0, 64, 1), a1)
            some = total > 0.0
            safe = jnp.where(some, total, 1.0)
            values[rows] = (numer / safe).astype(BF16)
            high = jnp.where(first, best[0, s, rows], best[1, s, rows])
            lse = jnp.where(some, high + jnp.log(safe) * LOG2E, LOW).T
            stats[0:8, rows] = lse[0:8]
            stats[8:16, rows] = lse[64:72]

    o_copies = []
    for k in range(1, NY):
        s = (y + k) % NY
        partial(s, otx.at[k - 1], stx.at[k - 1])
        device = at(s, z, xh, mp)
        for copy in (
            remote(otx.at[k - 1], orx.at[y], o_send.at[k - 1], o_recv.at[y], device),
            remote(stx.at[k - 1], srx.at[y], s_send.at[k - 1], s_recv.at[y], device),
        ):
            copy.start()
            o_copies.append(copy)
    partial(y, orx.at[y], srx.at[y])
    for k in range(1, NY):
        s = (y + k) % NY
        remote(orx.at[s], orx.at[s], o_send.at[k - 1], o_recv.at[s], z_up).wait_recv()
        remote(srx.at[s], srx.at[s], s_send.at[k - 1], s_recv.at[s], z_up).wait_recv()
    for r in range(ROWS // CHUNK):
        rows = pl.ds(r * CHUNK, CHUNK)
        lses = []
        for s in range(NY):
            pair = [
                jnp.broadcast_to(srx[s, 8 * h : 8 * h + 1, rows], (64, CHUNK)) for h in range(2)
            ]
            lses.append(jnp.concatenate(pair, axis=0).T)
        top = jnp.maximum(jnp.maximum(lses[0], lses[1]), jnp.maximum(lses[2], lses[3]))
        numer = jnp.zeros((CHUNK, 128), F32)
        denom = jnp.zeros((CHUNK, 128), F32)
        for s in range(NY):
            weight = jnp.exp2(lses[s] - top)
            denom = denom + weight
            numer = numer + weight * orx[s, rows].astype(F32)
        att[rows] = (numer / denom).astype(BF16)

    column = 2 * mp + xh
    a_copies = []
    for k in range(1, 8):
        e, device = group_member(k)
        src = att.at[pl.ds(pl.multiple_of(e * SUB, 16), SUB)]
        copy = remote(src, slices.at[column], a_send.at[k - 1], a_recv.at[column], device)
        copy.start()
        a_copies.append(copy)
    slices[column] = att[pl.ds(pl.multiple_of(mine * SUB, 16), SUB)]
    for k in range(1, 8):
        e = (mine + k) % 8
        source = 2 * (e % 4) + e // 4
        remote(
            slices.at[source], slices.at[source], a_send.at[k - 1], a_recv.at[source], sibling
        ).wait_recv()
    for i, (src, dst) in enumerate(weights):
        w_copies[i].wait()
        near = dst.at[xl * 2 + 1 - core]
        remote(src, near, w_send.at[i, 2], w_recv.at[i, 2], sibling).wait_recv()
        away = dst.at[(1 - xl) * 2 + 1 - core]
        remote(away, away, w_send.at[i, 3], w_recv.at[i, 3], sibling).wait_recv()

    total = xbuf[pl.ds(pl.multiple_of(own_rows + mp * SUB, 16), SUB)].astype(F32)
    for m in range(4):
        pair = jnp.concatenate([slices[2 * m], slices[2 * m + 1]], axis=1)
        total = total + jnp.dot(pair, wo[m], preferred_element_type=F32)
    resid = total.astype(BF16).astype(F32)
    mlp_in = rms(resid, gain_mlp[...]).astype(BF16)
    outcome = resid
    for m in range(4):
        hidden = jnp.dot(mlp_in, wu[m], preferred_element_type=F32)
        hidden = jax.nn.gelu(hidden, approximate=True).astype(BF16)
        outcome = outcome + jnp.dot(hidden, wd[m], preferred_element_type=F32)
    rbuf[mp] = rms(outcome, gain_read[...]).astype(BF16)

    def r_copy(slot, i, device):
        return remote(rbuf.at[slot], rbuf.at[slot], r_send.at[i], r_recv.at[i], device)

    r_copy(mp, 0, beside).start()
    r_copy(mp, 1, sibling).start()
    r_copy(xl * 2 + 1 - core, 1, sibling).wait_recv()
    for copy in late:
        copy.wait()
    terms[...] = jnp.zeros_like(terms)

    def readout(chip):
        rows = pl.ds(pl.multiple_of(chip * (2 * SUB), 32), 2 * SUB)
        read_in[...] = jnp.concatenate([rbuf[2 * chip], rbuf[2 * chip + 1]], axis=0)

        def columns_of(t, carry):
            tile = pl.ds(pl.multiple_of(t * TILE, TILE), TILE)
            rate = jnp.dot(read_in[...], wread[:, tile], preferred_element_type=F32)
            rate = rate + bias[:, tile]
            out[rows, tile] = rate.astype(BF16)
            term = jnp.exp(rate) - spikes[rows, tile].astype(F32) * rate
            folded = term[:, 0:128]
            for i in range(1, TILE // 128):
                folded = folded + term[:, i * 128 : (i + 1) * 128]
            terms[rows] = terms[rows] + folded
            return carry

        lax.fori_loop(0, wread.shape[1] // TILE, columns_of, 0)

    readout(xl)
    r_copy(theirs, 0, beside).wait_recv()
    r_copy(theirs, 2, sibling).start()
    r_copy((1 - xl) * 2 + 1 - core, 2, sibling).wait_recv()
    readout(1 - xl)
    for r in range(3):
        rows = pl.ds(r * 128, 128)
        part = jnp.sum(terms[rows].T, axis=0, keepdims=True)
        lossbuf[mp, :, rows] = jnp.broadcast_to(part, (8, 128))
    t_copies = []
    for k in range(1, 4):
        copy = remote(
            lossbuf.at[mp], lossbuf.at[mp], t_send.at[k - 1], t_recv.at[mp], at(y, z, xh, (mp + k) % 4)
        )
        copy.start()
        t_copies.append(copy)
    for k in range(1, 4):
        m = (mp + k) % 4
        remote(lossbuf.at[m], lossbuf.at[m], t_send.at[k - 1], t_recv.at[m], sibling).wait_recv()
    summed = (lossbuf[0] + lossbuf[1]) + (lossbuf[2] + lossbuf[3])
    loss[...] = summed[0:1, 0 : 4 * SUB] / NEU

    x_cross.wait_send()
    x_forward.wait_send()
    m_copy.wait_send()
    for copy in q_copies + o_copies + a_copies + t_copies:
        copy.wait_send()
    for d in range(4):
        for h in range(2):
            for direction in range(2):
                if d < 3 or h == direction:
                    kv_copy(h, z, direction, d).wait_send()
    for i, (src, dst) in enumerate(weights):
        rows = src.shape[0]
        for j in range(2):
            part = pl.ds(j * (rows // 2), rows // 2)
            remote(
                src.at[part], dst.at[mp, part], w_send.at[i, j], w_recv.at[i, j], sibling
            ).wait_send()
        remote(src, dst.at[mp], w_send.at[i, 2], w_recv.at[i, 2], sibling).wait_send()
        remote(
            dst.at[theirs], dst.at[theirs], w_send.at[i, 3], w_recv.at[i, 3], sibling
        ).wait_send()
    r_copy(mp, 0, beside).wait_send()
    r_copy(mp, 1, sibling).wait_send()
    r_copy(theirs, 2, sibling).wait_send()


def layer(gains, bias, stream, wq, wk, wv, wo, wu, wd, read_weight, spikes):
    vmem = pl.BlockSpec(memory_space=pltpu.VMEM)
    hbm = pl.BlockSpec(memory_space=pl.ANY)
    dma = pltpu.SemaphoreType.DMA
    return pl.pallas_call(
        layer_kernel,
        out_shape=(
            jax.ShapeDtypeStruct(spikes.shape, BF16),
            jax.ShapeDtypeStruct((1, spikes.shape[0]), F32),
        ),
        in_specs=[vmem] * 4 + [hbm] * 9,
        out_specs=(vmem, vmem),
        scratch_shapes=[
            pltpu.VMEM((WIDE, 128), BF16),
            pltpu.VMEM((WIDE, 128), BF16),
            pltpu.VMEM((WIDE, 128), BF16),
            pltpu.VMEM(read_weight.shape, BF16),
            pltpu.VMEM(spikes.shape, jnp.int32),
            pltpu.VMEM((2 * SUB, WIDE), BF16),
            pltpu.VMEM((384, 128), F32),
            pltpu.VMEM((4, 8, 384), F32),
            pltpu.VMEM((ROWS, WIDE), BF16),
            pltpu.VMEM((2, NZ, 128, ROWS), BF16),
            pltpu.VMEM((128, ROWS), BF16),
            pltpu.VMEM((128, ROWS), BF16),
            pltpu.VMEM((NY, ROWS, 128), BF16),
            pltpu.VMEM((2, NY, ROWS, 128), BF16),
            pltpu.VMEM((2, NY, ROWS, 128), F32),
            pltpu.VMEM((2, NY, ROWS, 128), F32),
            pltpu.VMEM((NY - 1, ROWS, 128), BF16),
            pltpu.VMEM((NY, ROWS, 128), BF16),
            pltpu.VMEM((NY - 1, 16, ROWS), F32),
            pltpu.VMEM((NY, 16, ROWS), F32),
            pltpu.VMEM((ROWS, 128), BF16),
            pltpu.VMEM((8, SUB, 128), BF16),
            pltpu.VMEM((4,) + wo.shape, BF16),
            pltpu.VMEM((4,) + wu.shape, BF16),
            pltpu.VMEM((4,) + wd.shape, BF16),
            pltpu.VMEM((4, SUB, WIDE), BF16),
            dma((2,)),
            dma((2,)),
            dma((2, 2, 4)),
            dma((2, NZ)),
            dma,
            dma,
            dma((NY - 1,)),
            dma((NY,)),
            dma((NY - 1,)),
            dma((NY,)),
            dma((NY - 1,)),
            dma((NY,)),
            dma((7,)),
            dma((8,)),
            dma((3,)),
            dma((3, 4)),
            dma((3, 4)),
            dma((3,)),
            dma((3,)),
            dma((3,)),
            dma((4,)),
            dma((6,)),
        ],
        compiler_params=pltpu.CompilerParams(
            collective_id=0, has_side_effects=True, vmem_limit_bytes=60 * 1024 * 1024
        ),
    )(*gains, bias, stream, wq, wk, wv, wo, wu, wd, read_weight, spikes)


def per_device(
    stream,
    gain_attn,
    gain_mlp,
    gain_read,
    query_weight,
    key_weight,
    value_weight,
    out_weight,
    up_weight,
    down_weight,
    read_weight,
    read_bias,
    spike_counts,
):
    gains = [gain.reshape(1, WIDE) for gain in (gain_attn, gain_mlp, gain_read)]
    log_rate, poisson_loss = layer(
        gains,
        read_bias.reshape(1, -1),
        stream,
        query_weight,
        key_weight,
        value_weight,
        out_weight,
        up_weight,
        down_weight,
        read_weight,
        spike_counts,
    )
    return (log_rate, poisson_loss.reshape(-1))


def solution(mesh):
    in_specs = (
        P("seq", None),
        P(),
        P(),
        P(),
        P(None, "mp"),
        P(None, "mp"),
        P(None, "mp"),
        P("mp", None),
        P(None, "mp"),
        P("mp", None),
        P(None, "mp"),
        P("mp"),
        P("seq", "mp"),
    )
    out_specs = (P("seq", "mp"), P("seq"))
    return jax.shard_map(
        per_device, mesh=mesh, in_specs=in_specs, out_specs=out_specs, check_vma=False
    )
```
